256 devices in a mesh: snap: 32 (over z_hi, x, y), vert: 8 (over z_lo, core).
Axes of the slice: x: 4, y: 4, z: 8 (z_hi: 2, z_lo: 4; z = z_hi * 4 + z_lo), core: 2. Of those that a mesh axis runs over, the one named last changes fastest.
Arguments:
- features: bfloat16 [64, 8192, 128], P('snap', 'vert'), may hold values from -6 to 6
- tile_cols: int32 [64, 64, 8], P('snap', 'vert'), may hold values from 0 to 63
- tile_weights: int32 [64, 64, 8, 128, 128], P('snap', 'vert'), may hold values from 0 to 3
- graph_gain: float32 [2, 128], replicated, may hold values from 0.5 to 1.5
- graph_up: bfloat16 [2, 128, 512], replicated, may hold values from -0.5 to 0.5
- graph_down: bfloat16 [2, 512, 128], replicated, may hold values from -0.25 to 0.25
- lag_mix: float32 [2, 8, 128], replicated, may hold values from -2 to 2
- time_gain: float32 [2, 128], replicated, may hold values from 0.5 to 1.5
- time_up: bfloat16 [2, 128, 1024], replicated, may hold values from -0.5 to 0.5
- time_down: bfloat16 [2, 1024, 128], replicated, may hold values from -0.1875 to 0.1875
Outputs:
- result: bfloat16 [64, 8192, 128], P('snap', 'vert')
The draws below stay inside these ranges and needn't reach their ends.
All inputs are finite; a program needn't handle non-finite values.
Results may differ from the reference program's by a relative error of at most 0.0085.
Values may be sent and summed in bfloat16 or wider, within the bound.
No kernel may reach another device: no remote copies, remote signals or barrier semaphores. Data moves between devices by JAX's collectives and lax.ppermute only.
A program may use at most 64 MiB of HBM per device.

```python
import jax
import jax.numpy as jnp
from jax import lax

F = 128
HG = 512
HT = 1024
TILE = 128
K = 8
LAGS = 8
LAYERS = 2
SNAPS = 64
VERTS = 8192


def with_ends(drawn, stream_key, least, high):
    spot = [jax.random.randint(jax.random.fold_in(stream_key, axis), (), 0, length) for axis, length in enumerate(drawn.shape)]
    longest = drawn.shape.index(max(drawn.shape))
    neighbour = spot[:longest] + [(spot[longest] + 1) % drawn.shape[longest]] + spot[longest + 1:]
    return drawn.at[tuple(spot)].set(least).at[tuple(neighbour)].set(high)


def block_levels(rng, shape, split, low, high):
    def one(position, blocks):
        heights = jax.random.uniform(jax.random.fold_in(jax.random.fold_in(rng, 6), position), (blocks,), jnp.float32, low / len(split), high / len(split))
        return jnp.repeat(jnp.exp(heights), shape[position] // blocks).reshape((-1,) + (1,) * (len(shape) - position - 1))

    gain = one(*split[0])
    for cut in split[1:]:
        gain = gain * one(*cut)
    return gain


def gaussian(key, extent, scale, bound, pieces=(), held_as=jnp.bfloat16):
    drawn = jax.random.normal(key, extent, jnp.float32) * scale
    if len(pieces) > 0:
        drawn = block_levels(key, extent, pieces, -0.22, 0.18) * drawn
    return jnp.clip(drawn, min=-bound, max=bound).astype(held_as)


def setup_inputs(seed: int = 0) -> dict:
    key_of = jax.random.split(jax.random.key(seed), 11)
    features = gaussian(key_of[0], (SNAPS, VERTS, F), 1.0, 6.0, ((0, 32), (1, 8)))
    tile_cols = with_ends(jax.random.randint(key_of[1], (SNAPS, VERTS // TILE, K), 0, VERTS // TILE), jax.random.fold_in(key_of[1], 1), 0, (VERTS // TILE) - 1).astype(jnp.int32)
    tile_weights = with_ends(jax.random.randint(key_of[2], (SNAPS, VERTS // TILE, K, TILE, TILE), 0, 4), jax.random.fold_in(key_of[2], 1), 0, 3).astype(jnp.int32)
    graph_gain = jnp.clip(1.0 + 0.1 * jax.random.normal(key_of[3], (LAYERS, F), jnp.float32), 0.5, 1.5)
    graph_up = gaussian(key_of[4], (LAYERS, F, HG), F ** -0.5, 0.5)
    graph_down = gaussian(key_of[5], (LAYERS, HG, F), HG ** -0.5, 0.25)
    lag_mix = gaussian(key_of[6], (LAYERS, LAGS, F), LAGS ** -0.5, 2.0, (), jnp.float32)
    time_gain = jnp.clip(1.0 + 0.1 * jax.random.normal(key_of[7], (LAYERS, F), jnp.float32), 0.5, 1.5)
    time_up = gaussian(key_of[8], (LAYERS, F, HT), F ** -0.5, 0.5)
    time_down = gaussian(key_of[9], (LAYERS, HT, F), HT ** -0.5, 0.1875)
    return dict(features=features, tile_cols=tile_cols, tile_weights=tile_weights, graph_gain=graph_gain, graph_up=graph_up, graph_down=graph_down, lag_mix=lag_mix, time_gain=time_gain, time_up=time_up, time_down=time_down)


eps = 1e-06

def rms_scale(activation, gain_row):
    return activation * lax.rsqrt(lax.optimization_barrier(jnp.mean(activation * activation, axis=-1, keepdims=True)) + eps) * gain_row

def mlp_branch(residual, mixed_rows, gain_row, up_weight, down_weight):
    feature_width = residual.shape[-1]
    normed = rms_scale(mixed_rows, gain_row).astype(jnp.bfloat16).reshape(-1, feature_width)
    hidden = jax.nn.gelu(jnp.dot(normed, up_weight, preferred_element_type=jnp.float32)).astype(jnp.bfloat16)
    branch = jnp.dot(hidden, down_weight, preferred_element_type=jnp.float32).reshape(residual.shape)
    return (residual.astype(jnp.float32) + branch).astype(jnp.bfloat16)

def lagged(sequence, lag_rows, before, out_count):
    widened = sequence.astype(jnp.float32)
    running = jnp.zeros((out_count,) + sequence.shape[1:], jnp.float32)
    for lag_step in range(lag_rows.shape[0]):
        running = running + lag_rows[lag_step] * lax.slice_in_dim(widened, before - lag_step, before - lag_step + out_count, axis=0)
    return running

def aggregate(snapshot, columns, blocks):
    feature_width = snapshot.shape[-1]
    stacked = snapshot.reshape(-1, TILE, feature_width)
    picked = stacked[columns]
    product = jnp.einsum('rkij,rkjf->rif', blocks.astype(jnp.float32), picked.astype(jnp.float32))
    return product.reshape(-1, feature_width)

def reference(features, tile_cols, tile_weights, graph_gain, graph_up, graph_down, lag_mix, time_gain, time_up, time_down):
    state = features
    for layer_index in range(LAYERS):

        def one_snapshot(operands):
            return aggregate(operands[0], operands[1], operands[2])
        summed = lax.map(one_snapshot, (state, tile_cols, tile_weights))
        graph_out = mlp_branch(state, summed, graph_gain[layer_index], graph_up[layer_index], graph_down[layer_index])
        padded = jnp.concatenate([jnp.zeros((LAGS - 1,) + graph_out.shape[1:], jnp.bfloat16), graph_out], axis=0)
        mixed_rows = lagged(padded, lag_mix[layer_index], LAGS - 1, SNAPS)
        state = mlp_branch(graph_out, mixed_rows, time_gain[layer_index], time_up[layer_index], time_down[layer_index])
    return state
```

```python
import functools

import jax
import jax.numpy as jnp
from jax import lax
from jax.experimental import pallas as pl
from jax.experimental.pallas import tpu as pltpu
from jax.sharding import Mesh, PartitionSpec as P

EPS = 1e-06
AXES = ("zh", "x", "y", "zl", "co")
PLANE = ("x", "y")
LINE = ("zl", "co")


def gelu(x):
    inner = 0.7978845608028654 * (x + 0.044715 * (x * x * x))
    return (0.5 * x) * (1.0 + jnp.tanh(inner))


def rms(x, gain):
    scale = lax.rsqrt(jnp.mean(x * x, axis=-1, keepdims=True) + EPS)
    return (x * scale * gain).astype(jnp.bfloat16)


def mlp(residual, rows, gain, up, down):
    hidden = gelu(
        jnp.dot(rms(rows, gain), up, preferred_element_type=jnp.float32)
    ).astype(jnp.bfloat16)
    branch = jnp.dot(hidden, down, preferred_element_type=jnp.float32)
    return (residual.astype(jnp.float32) + branch).astype(jnp.bfloat16)


def graph_kernel(layer, chips, steps, blocked, *refs):
    place, cols, own, mate = refs[:4]
    pieces = refs[4 : 4 + 4 * steps]
    weights, gain, up, down, out, state, tiles, summed, state_sem, tile_sem = refs[
        4 + 4 * steps :
    ]
    z, c = place[0], place[1]
    snaps, row_tiles, k_count = cols.shape
    span = out.shape[0]
    half = out.shape[2]
    tile = 2 * half

    def move(piece, slot):
        for t in range(snaps):
            pltpu.make_async_copy(
                piece.at[:, t] if blocked else piece.at[t],
                state.at[t, pl.ds(slot * span, span)],
                state_sem.at[t, slot],
            ).start()

    move(own, 2 * z + c)
    move(mate, 2 * z + 1 - c)
    for step in range(1, steps + 1):
        ahead, behind, ahead_mate, behind_mate = pieces[4 * (step - 1) : 4 * step]
        shift = step * (1 - 2 * c)

        def place_pair(mine, other, chip):
            @pl.when(jnp.logical_and(chip >= 0, chip < chips))
            def _():
                move(mine, 2 * chip + c)
                move(other, 2 * chip + 1 - c)

        place_pair(ahead, behind_mate, z - shift)
        place_pair(behind, ahead_mate, z + shift)

    def tile_copy(t):
        return pltpu.make_async_copy(weights.at[t], tiles.at[t], tile_sem.at[t])

    for t in range(snaps):
        tile_copy(t).start()
    for t in range(snaps):
        for slot in range(2 * chips):
            pltpu.make_async_copy(
                own.at[:, t] if blocked else own.at[t],
                state.at[t, pl.ds(slot * span, span)],
                state_sem.at[t, slot],
            ).wait()
        tile_copy(t).wait()
        for r in range(row_tiles):
            picked = jnp.concatenate(
                [
                    state[t, pl.ds(2 * cols[t, r, k], 2)].reshape(tile, tile)
                    for k in range(k_count)
                ],
                axis=0,
            )
            summed[pl.ds(r * tile, tile)] = jnp.dot(
                tiles[t, r], picked, preferred_element_type=jnp.float32
            )
        chunk = 512
        for q in range(row_tiles * tile // chunk):
            blocks = chunk // half
            residual = state[t, pl.ds((2 * z + c) * span + q * blocks, blocks)]
            done = mlp(
                residual.reshape(chunk, tile),
                summed[pl.ds(q * chunk, chunk)],
                gain[layer],
                up[layer],
                down[layer],
            )
            out[pl.ds(q * blocks, blocks), t] = done.reshape(blocks, half, tile)


def graph_stage(layer, blocked, place, cols, own, mate, pieces, weights, gain, up, down):
    steps = len(pieces) // 4
    chips = steps + 1
    snaps, row_tiles, k_count = cols.shape
    width = own.shape[-1]
    span = row_tiles * 2
    half = width // 2
    any_spec = pl.BlockSpec(memory_space=pl.ANY)
    smem = pl.BlockSpec(memory_space=pltpu.SMEM)
    vmem = pl.BlockSpec(memory_space=pltpu.VMEM)
    return pl.pallas_call(
        functools.partial(graph_kernel, layer, chips, steps, blocked),
        out_shape=jax.ShapeDtypeStruct((span, snaps, half, width), jnp.bfloat16),
        in_specs=[smem, smem]
        + [any_spec] * (3 + len(pieces))
        + [vmem] * 3,
        out_specs=pl.BlockSpec(memory_space=pltpu.VMEM),
        scratch_shapes=[
            pltpu.VMEM((snaps, 2 * chips * span, half, width), jnp.bfloat16),
            pltpu.VMEM(weights.shape, jnp.bfloat16),
            pltpu.VMEM((row_tiles * width, width), jnp.float32),
            pltpu.SemaphoreType.DMA((snaps, 2 * chips)),
            pltpu.SemaphoreType.DMA((snaps,)),
        ],
        compiler_params=pltpu.CompilerParams(vmem_limit_bytes=40 << 20),
        name="graph",
    )(place, cols, own, mate, *pieces, weights, gain, up, down)


def time_kernel(layer, own, halo, lags, gain, up, down, out, ext, sem):
    before = halo.shape[0]
    snaps, rows, width = own.shape
    first = pltpu.make_async_copy(halo, ext.at[pl.ds(0, before)], sem.at[0])
    second = pltpu.make_async_copy(own, ext.at[pl.ds(before, snaps)], sem.at[1])
    first.start()
    second.start()
    first.wait()
    second.wait()
    group = 8
    for q in range(snaps // group):
        mixed = jnp.zeros((group, rows, width), jnp.float32)
        for m in range(before + 1):
            part = ext[pl.ds(before + q * group - m, group)].astype(jnp.float32)
            mixed = mixed + lags[layer, m].reshape(1, 1, width) * part
        residual = ext[pl.ds(before + q * group, group)]
        done = mlp(
            residual.reshape(group * rows, width),
            mixed.reshape(group * rows, width),
            gain[layer],
            up[layer],
            down[layer],
        )
        out[pl.ds(q * group, group)] = done.reshape(group, rows, width)


def time_stage(layer, own, halo, lags, gain, up, down):
    snaps, rows, width = own.shape
    any_spec = pl.BlockSpec(memory_space=pl.ANY)
    vmem = pl.BlockSpec(memory_space=pltpu.VMEM)
    return pl.pallas_call(
        functools.partial(time_kernel, layer),
        out_shape=jax.ShapeDtypeStruct(own.shape, jnp.bfloat16),
        in_specs=[any_spec] * 2 + [vmem] * 4,
        out_specs=pl.BlockSpec(memory_space=pltpu.VMEM),
        scratch_shapes=[
            pltpu.VMEM((halo.shape[0] + snaps, rows, width), jnp.bfloat16),
            pltpu.SemaphoreType.DMA((2,)),
        ],
        compiler_params=pltpu.CompilerParams(vmem_limit_bytes=40 << 20),
        name="time",
    )(own, halo, lags, gain, up, down)


def line_paths(chips):
    climb = [(2 * z, 2 * z + 2) for z in range(chips - 1)]
    sink = [(2 * z + 3, 2 * z + 1) for z in range(chips - 1)]
    forward = climb + sink + [(2 * chips - 2, 2 * chips - 1), (1, 0)]
    return forward, [(b, a) for a, b in forward]


def gather_line(state):
    chips = lax.axis_size("zl")
    forward, backward = line_paths(chips)
    core = lax.axis_index("co")
    swap = lambda v: lax.ppermute(v, "co", [(0, 1), (1, 0)])
    mate = swap(state)
    ahead = behind = state
    pieces = []
    for _ in range(chips - 1):
        ahead = lax.ppermute(ahead, LINE, forward)
        behind = lax.ppermute(behind, LINE, backward)
        pieces.append((ahead, behind, swap(ahead), swap(behind)))
    return mate, pieces


def on_device(
    features,
    tile_cols,
    tile_weights,
    graph_gain,
    graph_up,
    graph_down,
    lag_mix,
    time_gain,
    time_up,
    time_down,
):
    snap_dev, vert_dev, width = features.shape
    row_tiles, k_count = tile_cols.shape[1:]
    owners = lax.axis_size(PLANE)
    half = vert_dev // owners
    lag_count = lag_mix.shape[1]
    core = lax.axis_index("co")
    place = jnp.stack([lax.axis_index("zl"), core]).astype(jnp.int32)
    weights = (
        tile_weights.astype(jnp.bfloat16)
        .transpose(0, 1, 3, 2, 4)
        .reshape(snap_dev, row_tiles, width, k_count * width)
    )
    g_gain = graph_gain[:, None, :]
    t_gain = time_gain[:, None, :]
    state = features.reshape(snap_dev, owners, half, width)
    for layer in range(graph_up.shape[0]):
        mate, moved = gather_line(state)
        pieces = []
        for ahead, behind, ahead_mate, behind_mate in moved:
            pieces += [ahead, behind, ahead_mate, behind_mate]
        graph_out = graph_stage(
            layer,
            layer > 0,
            place,
            tile_cols,
            state,
            mate,
            pieces,
            weights,
            g_gain,
            graph_up,
            graph_down,
        )
        owned = lax.all_to_all(graph_out, PLANE, 0, 0, tiled=True)
        owned = owned.reshape(owners * snap_dev, half, width)
        halo = lax.ppermute(owned[1 - lag_count :], "zh", [(0, 1)])
        finished = time_stage(layer, owned, halo, lag_mix, t_gain, time_up, time_down)
        state = lax.all_to_all(
            finished.reshape(owners, snap_dev, half, width), PLANE, 0, 0, tiled=True
        )
    return state.transpose(1, 0, 2, 3).reshape(snap_dev, vert_dev, width)


def solution(mesh):
    fine = Mesh(mesh.devices.reshape(2, 4, 4, 4, 2), AXES)
    snap, vert = ("zh", "x", "y"), LINE
    return jax.shard_map(
        on_device,
        mesh=fine,
        in_specs=(
            P(snap, vert, None),
            P(snap, vert, None),
            P(snap, vert, None, None, None),
        )
        + (P(),) * 7,
        out_specs=P(snap, vert, None),
        check_vma=False,
    )
```

```python
import functools

import jax
import jax.numpy as jnp
from jax import lax
from jax.experimental import pallas as pl
from jax.experimental.pallas import tpu as pltpu
from jax.sharding import Mesh, PartitionSpec as P

EPS = 1e-06
AXES = ("zh", "x", "y", "zl", "co")
OWNERS = ("x", "y")
LINE = ("zl", "co")


def rms(x, gain):
    scale = lax.rsqrt(jnp.mean(x * x, axis=-1, keepdims=True) + EPS)
    return (x * scale * gain).astype(jnp.bfloat16)


def mlp(residual, rows, gain, up, down):
    x = jnp.dot(rms(rows, gain), up, preferred_element_type=jnp.float32)
    inner = x * (0.7978845608028654 + 0.035677408136300125 * (x * x))
    doubled = (x + x * jnp.tanh(inner)).astype(jnp.bfloat16)
    branch = jnp.dot(doubled, down, preferred_element_type=jnp.float32)
    return (residual.astype(jnp.float32) + 0.5 * branch).astype(jnp.bfloat16)


def graph_kernel(layer, chips, blocked, near, *refs):
    count = 4 * chips - 2
    cols = refs[0]
    pieces = refs[1 : 1 + count]
    weights, gain, up, down, out, state, summed, sem = refs[1 + count :]
    z, c = lax.axis_index("zl"), lax.axis_index("co")
    snaps, row_tiles, k_count = cols.shape
    span, _, part, tile = out.shape
    per_tile = tile // part

    def fetch(piece, t, slot):
        return pltpu.make_async_copy(
            piece.at[:, t] if blocked else piece.at[t],
            state.at[t, pl.ds(slot * span, span)],
            sem.at[t, slot],
        )

    def place_piece(piece, slot):
        for t in range(snaps):
            if near:
                state[t, pl.ds(slot * span, span)] = piece[:, t] if blocked else piece[t]
            else:
                fetch(piece, t, slot).start()

    if near:
        for t in range(snaps):
            fetch(pieces[0], t, 2 * z + c).start()
    else:
        place_piece(pieces[0], 2 * z + c)
    place_piece(pieces[1], 2 * z + 1 - c)
    for step in range(1, chips):
        ahead, behind, ahead_mate, behind_mate = pieces[4 * step - 2 : 4 * step + 2]
        shift = step * (1 - 2 * c)

        def place_pair(mine, other, chip):
            @pl.when(jnp.logical_and(chip >= 0, chip < chips))
            def _():
                place_piece(mine, 2 * chip + c)
                place_piece(other, 2 * chip + 1 - c)

        place_pair(ahead, behind_mate, z - shift)
        place_pair(behind, ahead_mate, z + shift)

    for t in range(snaps):
        if near:
            fetch(pieces[0], t, 2 * z + c).wait()
        else:
            for slot in range(2 * chips):
                fetch(pieces[0], t, slot).wait()
    chunk = 512
    blocks = chunk // part

    @pl.loop(0, snaps)
    def _(t):
        for r in range(row_tiles):
            picked = jnp.concatenate(
                [
                    state[t, pl.ds(per_tile * cols[t, r, k], per_tile)].reshape(tile, tile)
                    for k in range(k_count)
                ],
                axis=0,
            )
            summed[pl.ds(r * tile, tile)] = jnp.dot(
                weights[t, r], picked, preferred_element_type=jnp.float32
            )
        for q in range(row_tiles * tile // chunk):
            residual = state[t, pl.ds((2 * z + c) * span + q * blocks, blocks)]
            done = mlp(
                residual.reshape(chunk, tile),
                summed[pl.ds(q * chunk, chunk)],
                gain[layer],
                up[layer],
                down[layer],
            )
            out[pl.ds(q * blocks, blocks), t] = done.reshape(blocks, part, tile)


def graph_stage(layer, cols, pieces, weights, gain, up, down):
    snaps, row_tiles, _ = cols.shape
    chips = (len(pieces) + 2) // 4
    part, width = pieces[0].shape[2:]
    span = row_tiles * width // part
    any_spec = pl.BlockSpec(memory_space=pl.ANY)
    smem = pl.BlockSpec(memory_space=pltpu.SMEM)
    vmem = pl.BlockSpec(memory_space=pltpu.VMEM)
    return pl.pallas_call(
        functools.partial(graph_kernel, layer, chips, layer > 0, True),
        out_shape=jax.ShapeDtypeStruct((span, snaps, part, width), jnp.bfloat16),
        in_specs=[smem, any_spec]
        + [vmem] * (len(pieces) - 1)
        + [vmem] * 4,
        out_specs=vmem,
        scratch_shapes=[
            pltpu.VMEM((snaps, 2 * chips * span, part, width), jnp.bfloat16),
            pltpu.VMEM((row_tiles * width, width), jnp.float32),
            pltpu.SemaphoreType.DMA((snaps, 2 * chips)),
        ],
        compiler_params=pltpu.CompilerParams(vmem_limit_bytes=12 << 20),
        name="graph",
    )(cols, *pieces, weights, gain, up, down)


def tie(value, other):
    any_spec = pl.BlockSpec(memory_space=pl.ANY)
    return pl.pallas_call(
        lambda *refs: None,
        out_shape=jax.ShapeDtypeStruct(value.shape, value.dtype),
        in_specs=[any_spec] * 2,
        out_specs=any_spec,
        input_output_aliases={0: 0},
        compiler_params=pltpu.CompilerParams(vmem_limit_bytes=1 << 18),
        name="tie",
    )(value, other)


GROUP = 8


def late_kernel(layer, own, lags, gain, up, down, out):
    before = lags.shape[1] - 1
    rows, width = own.shape[1:]
    for q in range(1, own.shape[0] // GROUP):
        mixed = jnp.zeros((GROUP, rows, width), jnp.float32)
        for m in range(before + 1):
            part = own[pl.ds(q * GROUP - m, GROUP)].astype(jnp.float32)
            mixed = mixed + lags[layer, m].reshape(1, 1, width) * part
        done = mlp(
            own[pl.ds(q * GROUP, GROUP)].reshape(GROUP * rows, width),
            mixed.reshape(GROUP * rows, width),
            gain[layer],
            up[layer],
            down[layer],
        )
        out[pl.ds(q * GROUP, GROUP)] = done.reshape(GROUP, rows, width)


def early_kernel(layer, own, halo, lags, gain, up, down, later, out, ext):
    before = halo.shape[0]
    rows, width = own.shape[1:]
    ext[pl.ds(0, before)] = jnp.where(lax.axis_index("zh") > 0, halo[...], jnp.zeros_like(halo))
    ext[pl.ds(before, GROUP)] = own[pl.ds(0, GROUP)]
    mixed = jnp.zeros((GROUP, rows, width), jnp.float32)
    for m in range(before + 1):
        part = ext[pl.ds(before - m, GROUP)].astype(jnp.float32)
        mixed = mixed + lags[layer, m].reshape(1, 1, width) * part
    done = mlp(
        own[pl.ds(0, GROUP)].reshape(GROUP * rows, width),
        mixed.reshape(GROUP * rows, width),
        gain[layer],
        up[layer],
        down[layer],
    )
    out[pl.ds(0, GROUP)] = done.reshape(GROUP, rows, width)


def time_stage(layer, own, lags, gain, up, down):
    before = lags.shape[1] - 1
    halo = lax.ppermute(own[-before:], "zh", [(0, 1), (1, 0)])
    vmem = pl.BlockSpec(memory_space=pltpu.VMEM)
    params = pltpu.CompilerParams(vmem_limit_bytes=4 << 20)
    out_shape = jax.ShapeDtypeStruct(own.shape, jnp.bfloat16)
    later = pl.pallas_call(
        functools.partial(late_kernel, layer),
        out_shape=out_shape,
        in_specs=[vmem] * 5,
        out_specs=vmem,
        compiler_params=params,
        name="late",
    )(own, lags, gain, up, down)
    return pl.pallas_call(
        functools.partial(early_kernel, layer),
        out_shape=out_shape,
        in_specs=[vmem] * 7,
        out_specs=vmem,
        scratch_shapes=[pltpu.VMEM((before + GROUP,) + own.shape[1:], jnp.bfloat16)],
        input_output_aliases={6: 0},
        compiler_params=params,
        name="early",
    )(own, halo, lags, gain, up, down, later)


def line_paths(chips):
    climb = [(2 * z, 2 * z + 2) for z in range(chips - 1)]
    sink = [(2 * z + 3, 2 * z + 1) for z in range(chips - 1)]
    forward = climb + sink + [(2 * chips - 2, 2 * chips - 1), (1, 0)]
    return forward, [(b, a) for a, b in forward]


def gather_line(state, beside=None):
    chips = lax.axis_size("zl")
    forward, backward = line_paths(chips)
    swap = lambda v: lax.ppermute(v, "co", [(0, 1), (1, 0)])
    ahead = state
    behind = state if beside is None else tie(state, beside)
    pieces = [state, swap(state)]
    for _ in range(chips - 1):
        ahead = lax.ppermute(ahead, LINE, forward)
        behind = lax.ppermute(behind, LINE, backward)
        pieces += [ahead, behind, swap(ahead), swap(behind)]
    return pieces


def on_device(
    features,
    tile_cols,
    tile_weights,
    graph_gain,
    graph_up,
    graph_down,
    lag_mix,
    time_gain,
    time_up,
    time_down,
):
    snaps, vert_dev, width = features.shape
    owners = lax.axis_size(OWNERS)
    part = vert_dev // owners
    g_gain = graph_gain[:, None, :]
    t_gain = time_gain[:, None, :]
    row_tiles, k_count = tile_cols.shape[1:]
    weights = (
        tile_weights.astype(jnp.bfloat16)
        .transpose(0, 1, 3, 2, 4)
        .reshape(snaps, row_tiles, width, k_count * width)
    )
    state = features.reshape(snaps, owners, part, width)
    for layer in range(graph_up.shape[0]):
        pieces = gather_line(state, weights if layer == 0 else None)
        graph_out = graph_stage(
            layer, tile_cols, pieces, weights, g_gain, graph_up, graph_down
        )
        owned = lax.all_to_all(graph_out, OWNERS, 0, 0, tiled=True)
        owned = owned.reshape(owners * snaps, part, width)
        finished = time_stage(layer, owned, lag_mix, t_gain, time_up, time_down)
        state = lax.all_to_all(
            finished.reshape(owners, snaps, part, width), OWNERS, 0, 0, tiled=True
        )
    return state.transpose(1, 0, 2, 3).reshape(snaps, vert_dev, width)


def solution(mesh):
    fine = Mesh(mesh.devices.reshape(2, 4, 4, 4, 2), AXES)
    snap, vert = ("zh", "x", "y"), LINE
    return jax.shard_map(
        on_device,
        mesh=fine,
        in_specs=(
            P(snap, vert, None),
            P(snap, vert, None),
            P(snap, vert, None, None, None),
        )
        + (P(),) * 7,
        out_specs=P(snap, vert, None),
        check_vma=False,
    )
```

```python
import functools

import jax
import jax.numpy as jnp
from jax import lax
from jax.experimental import pallas as pl
from jax.experimental.pallas import tpu as pltpu
from jax.sharding import Mesh, PartitionSpec as P

EPS = 1e-06
AXES = ("zh", "x", "y", "zl", "co")
OWNERS = ("x", "y")
LINE = ("zl", "co")


def rms(x, gain):
    scale = lax.rsqrt(jnp.mean(x * x, axis=-1, keepdims=True) + EPS)
    return (x * scale * gain).astype(jnp.bfloat16)


def mlp(residual, rows, gain, up, down):
    x = jnp.dot(rms(rows, gain), up, preferred_element_type=jnp.float32)
    inner = x * (0.7978845608028654 + 0.035677408136300125 * (x * x))
    doubled = (x + x * jnp.tanh(inner)).astype(jnp.bfloat16)
    branch = jnp.dot(doubled, down, preferred_element_type=jnp.float32)
    return (residual.astype(jnp.float32) + 0.5 * branch).astype(jnp.bfloat16)


def graph_kernel(layer, t, chips, *refs):
    count = 4 * chips - 2
    cols = refs[0]
    pieces = refs[1 : 1 + count]
    weights, gain, up, down = refs[1 + count : 5 + count]
    out, state, summed = refs[-3:]
    z, c = lax.axis_index("zl"), lax.axis_index("co")
    row_tiles, k_count = cols.shape[1:]
    span, _, part, tile = out.shape
    per_tile = tile // part

    def place_piece(piece, slot):
        state[pl.ds(slot * span, span)] = piece[...]

    place_piece(pieces[0], 2 * z + c)
    place_piece(pieces[1], 2 * z + 1 - c)
    for step in range(1, chips):
        ahead, behind, ahead_mate, behind_mate = pieces[4 * step - 2 : 4 * step + 2]
        shift = step * (1 - 2 * c)

        def place_pair(mine, other, chip):
            @pl.when(jnp.logical_and(chip >= 0, chip < chips))
            def _():
                place_piece(mine, 2 * chip + c)
                place_piece(other, 2 * chip + 1 - c)

        place_pair(ahead, behind_mate, z - shift)
        place_pair(behind, ahead_mate, z + shift)

    for r in range(row_tiles):
        picked = jnp.concatenate(
            [
                state[pl.ds(per_tile * cols[t, r, k], per_tile)].reshape(tile, tile)
                for k in range(k_count)
            ],
            axis=0,
        )
        summed[pl.ds(r * tile, tile)] = jnp.dot(
            weights[r], picked, preferred_element_type=jnp.float32
        )
    chunk = 512
    blocks = chunk // part

    for q in range(row_tiles * tile // chunk):
        done = mlp(
            pieces[0][pl.ds(q * blocks, blocks)].reshape(chunk, tile),
            summed[pl.ds(q * chunk, chunk)],
            gain[layer],
            up[layer],
            down[layer],
        )
        out[pl.ds(q * blocks, blocks), t] = done.reshape(blocks, part, tile)


def graph_stage(layer, cols, chunks, weights, gain, up, down):
    snaps, row_tiles, _ = cols.shape
    chips = (len(chunks[0]) + 2) // 4
    span, part, width = chunks[0][0].shape
    smem = pl.BlockSpec(memory_space=pltpu.SMEM)
    vmem = pl.BlockSpec(memory_space=pltpu.VMEM)
    result = []
    for t in range(snaps):
        operands = [cols, *chunks[t], weights[t], gain, up, down] + result
        result = [
            pl.pallas_call(
                functools.partial(graph_kernel, layer, t, chips),
                out_shape=jax.ShapeDtypeStruct((span, snaps, part, width), jnp.bfloat16),
                in_specs=[smem] + [vmem] * (len(operands) - 1),
                out_specs=vmem,
                scratch_shapes=[
                    pltpu.VMEM((2 * chips * span, part, width), jnp.bfloat16),
                    pltpu.VMEM((row_tiles * width, width), jnp.float32),
                ],
                input_output_aliases={len(operands) - 1: 0} if t > 0 else {},
                compiler_params=pltpu.CompilerParams(vmem_limit_bytes=8 << 20),
                name="graph",
            )(*operands)
        ]
    return result[0]


def tie(value, other):
    any_spec = pl.BlockSpec(memory_space=pl.ANY)
    return pl.pallas_call(
        lambda *refs: None,
        out_shape=jax.ShapeDtypeStruct(value.shape, value.dtype),
        in_specs=[any_spec] * 2,
        out_specs=any_spec,
        input_output_aliases={0: 0},
        compiler_params=pltpu.CompilerParams(vmem_limit_bytes=1 << 18),
        name="tie",
    )(value, other)


GROUP = 8


def late_kernel(layer, own, lags, gain, up, down, out):
    before = lags.shape[1] - 1
    rows, width = own.shape[1:]
    for q in range(1, own.shape[0] // GROUP):
        mixed = jnp.zeros((GROUP, rows, width), jnp.float32)
        for m in range(before + 1):
            part = own[pl.ds(q * GROUP - m, GROUP)].astype(jnp.float32)
            mixed = mixed + lags[layer, m].reshape(1, 1, width) * part
        done = mlp(
            own[pl.ds(q * GROUP, GROUP)].reshape(GROUP * rows, width),
            mixed.reshape(GROUP * rows, width),
            gain[layer],
            up[layer],
            down[layer],
        )
        out[pl.ds(q * GROUP, GROUP)] = done.reshape(GROUP, rows, width)


def early_kernel(layer, own, halo, lags, gain, up, down, later, out, ext):
    before = halo.shape[0]
    rows, width = own.shape[1:]
    ext[pl.ds(0, before)] = jnp.where(lax.axis_index("zh") > 0, halo[...], jnp.zeros_like(halo))
    ext[pl.ds(before, GROUP)] = own[pl.ds(0, GROUP)]
    mixed = jnp.zeros((GROUP, rows, width), jnp.float32)
    for m in range(before + 1):
        part = ext[pl.ds(before - m, GROUP)].astype(jnp.float32)
        mixed = mixed + lags[layer, m].reshape(1, 1, width) * part
    done = mlp(
        own[pl.ds(0, GROUP)].reshape(GROUP * rows, width),
        mixed.reshape(GROUP * rows, width),
        gain[layer],
        up[layer],
        down[layer],
    )
    out[pl.ds(0, GROUP)] = done.reshape(GROUP, rows, width)


def time_stage(layer, own, lags, gain, up, down):
    before = lags.shape[1] - 1
    halo = lax.ppermute(own[-before:], "zh", [(0, 1), (1, 0)])
    vmem = pl.BlockSpec(memory_space=pltpu.VMEM)
    params = pltpu.CompilerParams(vmem_limit_bytes=4 << 20)
    out_shape = jax.ShapeDtypeStruct(own.shape, jnp.bfloat16)
    later = pl.pallas_call(
        functools.partial(late_kernel, layer),
        out_shape=out_shape,
        in_specs=[vmem] * 5,
        out_specs=vmem,
        compiler_params=params,
        name="late",
    )(own, lags, gain, up, down)
    return pl.pallas_call(
        functools.partial(early_kernel, layer),
        out_shape=out_shape,
        in_specs=[vmem] * 7,
        out_specs=vmem,
        scratch_shapes=[pltpu.VMEM((before + GROUP,) + own.shape[1:], jnp.bfloat16)],
        input_output_aliases={6: 0},
        compiler_params=params,
        name="early",
    )(own, halo, lags, gain, up, down, later)


def line_paths(chips):
    climb = [(2 * z, 2 * z + 2) for z in range(chips - 1)]
    sink = [(2 * z + 3, 2 * z + 1) for z in range(chips - 1)]
    forward = climb + sink + [(2 * chips - 2, 2 * chips - 1), (1, 0)]
    return forward, [(b, a) for a, b in forward]


def gather_line(chunks, beside=()):
    chips = lax.axis_size("zl")
    forward, backward = line_paths(chips)
    swap = lambda v: lax.ppermute(v, "co", [(0, 1), (1, 0)])
    moved = [[chunk, swap(chunk)] for chunk in chunks]
    ahead, behind = list(chunks), list(chunks)
    for _ in range(chips - 1):
        for t in range(len(chunks)):
            ahead[t] = lax.ppermute(ahead[t], LINE, forward)
            behind[t] = lax.ppermute(behind[t], LINE, backward)
            if beside:
                behind[t] = tie(behind[t], beside.pop())
            moved[t] += [ahead[t], behind[t], swap(ahead[t]), swap(behind[t])]
    return moved


def on_device(
    features,
    tile_cols,
    tile_weights,
    graph_gain,
    graph_up,
    graph_down,
    lag_mix,
    time_gain,
    time_up,
    time_down,
):
    snaps, vert_dev, width = features.shape
    owners = lax.axis_size(OWNERS)
    part = vert_dev // owners
    g_gain = graph_gain[:, None, :]
    t_gain = time_gain[:, None, :]
    row_tiles, k_count = tile_cols.shape[1:]
    weights = [
        lax.optimization_barrier(tile_weights[t])
        .astype(jnp.bfloat16)
        .transpose(0, 2, 1, 3)
        .reshape(row_tiles, width, k_count * width)
        for t in range(snaps)
    ]
    chunks = [features[t].reshape(owners, part, width) for t in range(snaps)]
    for layer in range(graph_up.shape[0]):
        moved = gather_line(chunks, list(weights) if layer == 0 else [])
        graph_out = graph_stage(
            layer, tile_cols, moved, weights, g_gain, graph_up, graph_down
        )
        owned = lax.all_to_all(graph_out, OWNERS, 0, 0, tiled=True)
        owned = owned.reshape(owners * snaps, part, width)
        finished = time_stage(layer, owned, lag_mix, t_gain, time_up, time_down)
        state = lax.all_to_all(
            finished.reshape(owners, snaps, part, width), OWNERS, 0, 0, tiled=True
        )
        chunks = [state[:, t] for t in range(snaps)]
    return state.transpose(1, 0, 2, 3).reshape(snaps, vert_dev, width)


def solution(mesh):
    fine = Mesh(mesh.devices.reshape(2, 4, 4, 4, 2), AXES)
    snap, vert = ("zh", "x", "y"), LINE
    return jax.shard_map(
        on_device,
        mesh=fine,
        in_specs=(
            P(snap, vert, None),
            P(snap, vert, None),
            P(snap, vert, None, None, None),
        )
        + (P(),) * 7,
        out_specs=P(snap, vert, None),
        check_vma=False,
    )
```

```python
import functools

import jax
import jax.numpy as jnp
from jax import lax
from jax.experimental import pallas as pl
from jax.experimental.pallas import tpu as pltpu
from jax.sharding import Mesh, PartitionSpec as P

EPS = 1e-06
AXES = ("zh", "x", "y", "zl", "co")
OWNERS = ("x", "y")
LINE = ("zl", "co")


def rms(x, gain):
    scale = lax.rsqrt(jnp.mean(x * x, axis=-1, keepdims=True) + EPS)
    return (x * scale * gain).astype(jnp.bfloat16)


def mlp(residual, rows, gain, up, down):
    x = jnp.dot(rms(rows, gain), up, preferred_element_type=jnp.float32)
    inner = x * (0.7978845608028654 + 0.035677408136300125 * (x * x))
    doubled = (x + x * jnp.tanh(inner)).astype(jnp.bfloat16)
    branch = jnp.dot(doubled, down, preferred_element_type=jnp.float32)
    return (residual.astype(jnp.float32) + 0.5 * branch).astype(jnp.bfloat16)


def graph_kernel(layer, chips, blocked, *refs):
    cols, mate = refs[:2]
    snaps, row_tiles, k_count = cols.shape
    owns = refs[2 : 2 + snaps]
    moved = refs[2 + snaps : 2 + snaps + 2 * snaps * (chips - 1)]
    rest = refs[2 + snaps + 2 * snaps * (chips - 1) :]
    joined = rest[: chips - 1]
    weights, gain, up, down, out, state, summed = rest[chips - 1 :]
    z, c = lax.axis_index("zl"), lax.axis_index("co")
    span, _, part, tile = out.shape
    per_tile = tile // part

    def place(t, slot, value):
        state[t, pl.ds(slot * span, span)] = value

    for t in range(snaps):
        place(t, 2 * z + c, owns[t][...])
        place(t, 2 * z + 1 - c, mate[:, t] if blocked else mate[t])
    for step in range(1, chips):
        ahead = moved[2 * snaps * (step - 1) : 2 * snaps * (step - 1) + snaps]
        behind = moved[2 * snaps * (step - 1) + snaps : 2 * snaps * step]
        shift = step * (1 - 2 * c)

        @pl.when(jnp.logical_and(z - shift >= 0, z - shift < chips))
        def _():
            for t in range(snaps):
                other = joined[step - 1][snaps + t]
                place(t, 2 * (z - shift) + c, ahead[t][...])
                place(t, 2 * (z - shift) + 1 - c, other)

        @pl.when(jnp.logical_and(z + shift >= 0, z + shift < chips))
        def _():
            for t in range(snaps):
                other = joined[step - 1][t]
                place(t, 2 * (z + shift) + c, behind[t][...])
                place(t, 2 * (z + shift) + 1 - c, other)

    chunk = 512
    blocks = chunk // part

    @pl.loop(0, snaps)
    def _(t):
        for r in range(row_tiles):
            picked = jnp.concatenate(
                [
                    state[t, pl.ds(per_tile * cols[t, r, k], per_tile)].reshape(tile, tile)
                    for k in range(k_count)
                ],
                axis=0,
            )
            summed[pl.ds(r * tile, tile)] = jnp.dot(
                weights[t, r], picked, preferred_element_type=jnp.float32
            )
        for q in range(row_tiles * tile // chunk):
            residual = state[t, pl.ds((2 * z + c) * span + q * blocks, blocks)]
            done = mlp(
                residual.reshape(chunk, tile),
                summed[pl.ds(q * chunk, chunk)],
                gain[layer],
                up[layer],
                down[layer],
            )
            out[pl.ds(q * blocks, blocks), t] = done.reshape(blocks, part, tile)


def graph_stage(layer, cols, chips, pieces, weights, gain, up, down):
    snaps, row_tiles, _ = cols.shape
    span, part, width = pieces[1].shape
    smem = pl.BlockSpec(memory_space=pltpu.SMEM)
    vmem = pl.BlockSpec(memory_space=pltpu.VMEM)
    return pl.pallas_call(
        functools.partial(graph_kernel, layer, chips, layer > 0),
        out_shape=jax.ShapeDtypeStruct((span, snaps, part, width), jnp.bfloat16),
        in_specs=[smem] + [vmem] * (len(pieces) + 4),
        out_specs=vmem,
        scratch_shapes=[
            pltpu.VMEM((snaps, 2 * chips * span, part, width), jnp.bfloat16),
            pltpu.VMEM((row_tiles * width, width), jnp.float32),
        ],
        compiler_params=pltpu.CompilerParams(vmem_limit_bytes=12 << 20),
        name="graph",
    )(cols, *pieces, weights, gain, up, down)


def join(values):
    def kernel(*refs):
        for index, value in enumerate(refs[:-1]):
            refs[-1][index] = value[...]

    vmem = pl.BlockSpec(memory_space=pltpu.VMEM)
    return pl.pallas_call(
        kernel,
        out_shape=jax.ShapeDtypeStruct((len(values),) + values[0].shape, values[0].dtype),
        in_specs=[vmem] * len(values),
        out_specs=vmem,
        compiler_params=pltpu.CompilerParams(vmem_limit_bytes=1 << 20),
        name="join",
    )(*values)


def tie(value, other):
    any_spec = pl.BlockSpec(memory_space=pl.ANY)
    return pl.pallas_call(
        lambda *refs: None,
        out_shape=jax.ShapeDtypeStruct(value.shape, value.dtype),
        in_specs=[any_spec] * 2,
        out_specs=any_spec,
        input_output_aliases={0: 0},
        compiler_params=pltpu.CompilerParams(vmem_limit_bytes=1 << 18),
        name="tie",
    )(value, other)


GROUP = 8


def late_kernel(layer, own, lags, gain, up, down, out):
    before = lags.shape[1] - 1
    rows, width = own.shape[1:]
    @pl.loop(1, own.shape[0] // GROUP)
    def _(q):
        mixed = jnp.zeros((GROUP, rows, width), jnp.float32)
        for m in range(before + 1):
            part = own[pl.ds(q * GROUP - m, GROUP)].astype(jnp.float32)
            mixed = mixed + lags[layer, m].reshape(1, 1, width) * part
        done = mlp(
            own[pl.ds(q * GROUP, GROUP)].reshape(GROUP * rows, width),
            mixed.reshape(GROUP * rows, width),
            gain[layer],
            up[layer],
            down[layer],
        )
        out[pl.ds(q * GROUP, GROUP)] = done.reshape(GROUP, rows, width)


def early_kernel(layer, own, halo, lags, gain, up, down, later, out, ext):
    before = halo.shape[0]
    rows, width = own.shape[1:]
    ext[pl.ds(0, before)] = jnp.where(lax.axis_index("zh") > 0, halo[...], jnp.zeros_like(halo))
    ext[pl.ds(before, GROUP)] = own[pl.ds(0, GROUP)]
    mixed = jnp.zeros((GROUP, rows, width), jnp.float32)
    for m in range(before + 1):
        part = ext[pl.ds(before - m, GROUP)].astype(jnp.float32)
        mixed = mixed + lags[layer, m].reshape(1, 1, width) * part
    done = mlp(
        own[pl.ds(0, GROUP)].reshape(GROUP * rows, width),
        mixed.reshape(GROUP * rows, width),
        gain[layer],
        up[layer],
        down[layer],
    )
    out[pl.ds(0, GROUP)] = done.reshape(GROUP, rows, width)


def time_stage(layer, own, lags, gain, up, down):
    before = lags.shape[1] - 1
    halo = lax.ppermute(own[-before:], "zh", [(0, 1), (1, 0)])
    vmem = pl.BlockSpec(memory_space=pltpu.VMEM)
    params = pltpu.CompilerParams(vmem_limit_bytes=4 << 20)
    out_shape = jax.ShapeDtypeStruct(own.shape, jnp.bfloat16)
    later = pl.pallas_call(
        functools.partial(late_kernel, layer),
        out_shape=out_shape,
        in_specs=[vmem] * 5,
        out_specs=vmem,
        compiler_params=params,
        name="late",
    )(own, lags, gain, up, down)
    return pl.pallas_call(
        functools.partial(early_kernel, layer),
        out_shape=out_shape,
        in_specs=[vmem] * 7,
        out_specs=vmem,
        scratch_shapes=[pltpu.VMEM((before + GROUP,) + own.shape[1:], jnp.bfloat16)],
        input_output_aliases={6: 0},
        compiler_params=params,
        name="early",
    )(own, halo, lags, gain, up, down, later)


def line_paths(chips):
    climb = [(2 * z, 2 * z + 2) for z in range(chips - 1)]
    sink = [(2 * z + 3, 2 * z + 1) for z in range(chips - 1)]
    forward = climb + sink + [(2 * chips - 2, 2 * chips - 1), (1, 0)]
    return forward, [(b, a) for a, b in forward]


def gather_line(state, chunks, beside=None):
    chips = lax.axis_size("zl")
    forward, backward = line_paths(chips)
    swap = lambda v: lax.ppermute(v, "co", [(0, 1), (1, 0)])
    mate = swap(state)
    ahead, behind = list(chunks), list(chunks)
    moved, joined, last = [], [], []
    for step in range(1, chips):
        for t in range(len(chunks)):
            ahead[t] = lax.ppermute(ahead[t], LINE, forward)
            behind[t] = lax.ppermute(behind[t], LINE, backward)
        moved += ahead + behind
        if step < chips - 1:
            both = join(ahead + behind)
            if beside is not None:
                both, beside = tie(both, beside), None
            joined.append(swap(both))
        else:
            last = [swap(join(ahead + behind))]
    return [mate, *chunks, *moved, *joined, *last]


def on_device(
    features,
    tile_cols,
    tile_weights,
    graph_gain,
    graph_up,
    graph_down,
    lag_mix,
    time_gain,
    time_up,
    time_down,
):
    snaps, vert_dev, width = features.shape
    owners = lax.axis_size(OWNERS)
    part = vert_dev // owners
    g_gain = graph_gain[:, None, :]
    t_gain = time_gain[:, None, :]
    row_tiles, k_count = tile_cols.shape[1:]
    weights = (
        tile_weights.astype(jnp.bfloat16)
        .transpose(0, 1, 3, 2, 4)
        .reshape(snaps, row_tiles, width, k_count * width)
    )
    state = features.reshape(snaps, owners, part, width)
    chunks = [state[t] for t in range(snaps)]
    for layer in range(graph_up.shape[0]):
        pieces = gather_line(state, chunks, weights if layer == 0 else None)
        graph_out = graph_stage(
            layer, tile_cols, lax.axis_size("zl"), pieces, weights, g_gain, graph_up, graph_down
        )
        owned = lax.all_to_all(graph_out, OWNERS, 0, 0, tiled=True)
        owned = owned.reshape(owners * snaps, part, width)
        finished = time_stage(layer, owned, lag_mix, t_gain, time_up, time_down)
        state = lax.all_to_all(
            finished.reshape(owners, snaps, part, width), OWNERS, 0, 0, tiled=True
        )
        chunks = [state[:, t] for t in range(snaps)]
    return state.transpose(1, 0, 2, 3).reshape(snaps, vert_dev, width)


def solution(mesh):
    fine = Mesh(mesh.devices.reshape(2, 4, 4, 4, 2), AXES)
    snap, vert = ("zh", "x", "y"), LINE
    return jax.shard_map(
        on_device,
        mesh=fine,
        in_specs=(
            P(snap, vert, None),
            P(snap, vert, None),
            P(snap, vert, None, None, None),
        )
        + (P(),) * 7,
        out_specs=P(snap, vert, None),
        check_vma=False,
    )
```

```python
import functools

import jax
import jax.numpy as jnp
from jax import lax
from jax.experimental import pallas as pl
from jax.experimental.pallas import tpu as pltpu
from jax.sharding import Mesh, PartitionSpec as P

EPS = 1e-06
AXES = ("zh", "x", "y", "zl", "co")
OWNERS = ("x", "y")
LINE = ("zl", "co")


def rms(x, gain):
    scale = lax.rsqrt(jnp.mean(x * x, axis=-1, keepdims=True) + EPS)
    return (x * scale * gain).astype(jnp.bfloat16)


def mlp(residual, rows, gain, up, down):
    x = jnp.dot(rms(rows, gain), up, preferred_element_type=jnp.float32)
    inner = x * (0.7978845608028654 + 0.035677408136300125 * (x * x))
    doubled = (x + x * jnp.tanh(inner)).astype(jnp.bfloat16)
    branch = jnp.dot(doubled, down, preferred_element_type=jnp.float32)
    return (residual.astype(jnp.float32) + 0.5 * branch).astype(jnp.bfloat16)


def graph_kernel(layer, chips, blocked, *refs):
    cols, mate = refs[:2]
    snaps, row_tiles, k_count = cols.shape
    owns = refs[2 : 2 + snaps]
    moved = refs[2 + snaps : 2 + snaps + 2 * snaps * (chips - 1)]
    rest = refs[2 + snaps + 2 * snaps * (chips - 1) :]
    joined = rest[: chips - 1]
    weights, gain, up, down, out, state, summed = rest[chips - 1 :]
    z, c = lax.axis_index("zl"), lax.axis_index("co")
    span, _, part, tile = out.shape
    per_tile = tile // part

    def place(t, slot, value):
        state[t, pl.ds(slot * span, span)] = value

    for t in range(snaps):
        place(t, 2 * z + c, owns[t][...])
        place(t, 2 * z + 1 - c, mate[:, t] if blocked else mate[t])
    for step in range(1, chips):
        ahead = moved[2 * snaps * (step - 1) : 2 * snaps * (step - 1) + snaps]
        behind = moved[2 * snaps * (step - 1) + snaps : 2 * snaps * step]
        shift = step * (1 - 2 * c)

        @pl.when(jnp.logical_and(z - shift >= 0, z - shift < chips))
        def _():
            for t in range(snaps):
                other = joined[step - 1][t if 2 * step >= chips else snaps + t]
                place(t, 2 * (z - shift) + c, ahead[t][...])
                place(t, 2 * (z - shift) + 1 - c, other)

        @pl.when(jnp.logical_and(z + shift >= 0, z + shift < chips))
        def _():
            for t in range(snaps):
                other = joined[step - 1][t]
                place(t, 2 * (z + shift) + c, behind[t][...])
                place(t, 2 * (z + shift) + 1 - c, other)

    chunk = 512
    blocks = chunk // part

    @pl.loop(0, snaps)
    def _(t):
        for r in range(row_tiles):
            picked = jnp.concatenate(
                [
                    state[t, pl.ds(per_tile * cols[t, r, k], per_tile)].reshape(tile, tile)
                    for k in range(k_count)
                ],
                axis=0,
            )
            summed[pl.ds(r * tile, tile)] = jnp.dot(
                weights[t, r], picked, preferred_element_type=jnp.float32
            )
        for q in range(row_tiles * tile // chunk):
            residual = state[t, pl.ds((2 * z + c) * span + q * blocks, blocks)]
            done = mlp(
                residual.reshape(chunk, tile),
                summed[pl.ds(q * chunk, chunk)],
                gain[layer],
                up[layer],
                down[layer],
            )
            out[pl.ds(q * blocks, blocks), t] = done.reshape(blocks, part, tile)


def graph_stage(layer, cols, chips, pieces, weights, gain, up, down):
    snaps, row_tiles, _ = cols.shape
    span, part, width = pieces[1].shape
    smem = pl.BlockSpec(memory_space=pltpu.SMEM)
    vmem = pl.BlockSpec(memory_space=pltpu.VMEM)
    return pl.pallas_call(
        functools.partial(graph_kernel, layer, chips, layer > 0),
        out_shape=jax.ShapeDtypeStruct((span, snaps, part, width), jnp.bfloat16),
        in_specs=[smem] + [vmem] * (len(pieces) + 4),
        out_specs=vmem,
        scratch_shapes=[
            pltpu.VMEM((snaps, 2 * chips * span, part, width), jnp.bfloat16),
            pltpu.VMEM((row_tiles * width, width), jnp.float32),
        ],
        compiler_params=pltpu.CompilerParams(vmem_limit_bytes=12 << 20),
        name="graph",
    )(cols, *pieces, weights, gain, up, down)


def join(ahead, behind, step, chips):
    snaps = len(ahead)
    one_way = 2 * step >= chips

    def kernel(*refs):
        out = refs[-1]

        def put(first, values):
            for index, value in enumerate(values):
                out[first + index] = value[...]

        if one_way:
            source = lax.axis_index("zl") - step * (1 - 2 * lax.axis_index("co"))
            from_ahead = jnp.logical_and(source >= 0, source < chips)
            pl.when(from_ahead)(lambda: put(0, refs[:snaps]))
            pl.when(jnp.logical_not(from_ahead))(lambda: put(0, refs[snaps:-1]))
        else:
            put(0, refs[:-1])

    count = snaps if one_way else 2 * snaps
    vmem = pl.BlockSpec(memory_space=pltpu.VMEM)
    return pl.pallas_call(
        kernel,
        out_shape=jax.ShapeDtypeStruct((count,) + ahead[0].shape, ahead[0].dtype),
        in_specs=[vmem] * (2 * snaps),
        out_specs=vmem,
        compiler_params=pltpu.CompilerParams(vmem_limit_bytes=1 << 20),
        name="join",
    )(*ahead, *behind)


def tie(value, other):
    any_spec = pl.BlockSpec(memory_space=pl.ANY)
    return pl.pallas_call(
        lambda *refs: None,
        out_shape=jax.ShapeDtypeStruct(value.shape, value.dtype),
        in_specs=[any_spec] * 2,
        out_specs=any_spec,
        input_output_aliases={0: 0},
        compiler_params=pltpu.CompilerParams(vmem_limit_bytes=1 << 18),
        name="tie",
    )(value, other)


GROUP = 8


def late_kernel(layer, own, lags, gain, up, down, out):
    before = lags.shape[1] - 1
    rows, width = own.shape[1:]
    @pl.loop(1, own.shape[0] // GROUP)
    def _(q):
        mixed = jnp.zeros((GROUP, rows, width), jnp.float32)
        for m in range(before + 1):
            part = own[pl.ds(q * GROUP - m, GROUP)].astype(jnp.float32)
            mixed = mixed + lags[layer, m].reshape(1, 1, width) * part
        done = mlp(
            own[pl.ds(q * GROUP, GROUP)].reshape(GROUP * rows, width),
            mixed.reshape(GROUP * rows, width),
            gain[layer],
            up[layer],
            down[layer],
        )
        out[pl.ds(q * GROUP, GROUP)] = done.reshape(GROUP, rows, width)


def early_kernel(layer, own, halo, lags, gain, up, down, later, out, ext):
    before = halo.shape[0]
    rows, width = own.shape[1:]
    ext[pl.ds(0, before)] = jnp.where(lax.axis_index("zh") > 0, halo[...], jnp.zeros_like(halo))
    ext[pl.ds(before, GROUP)] = own[pl.ds(0, GROUP)]
    mixed = jnp.zeros((GROUP, rows, width), jnp.float32)
    for m in range(before + 1):
        part = ext[pl.ds(before - m, GROUP)].astype(jnp.float32)
        mixed = mixed + lags[layer, m].reshape(1, 1, width) * part
    done = mlp(
        own[pl.ds(0, GROUP)].reshape(GROUP * rows, width),
        mixed.reshape(GROUP * rows, width),
        gain[layer],
        up[layer],
        down[layer],
    )
    out[pl.ds(0, GROUP)] = done.reshape(GROUP, rows, width)


def time_stage(layer, own, lags, gain, up, down):
    before = lags.shape[1] - 1
    halo = lax.ppermute(own[-before:], "zh", [(0, 1), (1, 0)])
    vmem = pl.BlockSpec(memory_space=pltpu.VMEM)
    params = pltpu.CompilerParams(vmem_limit_bytes=4 << 20)
    out_shape = jax.ShapeDtypeStruct(own.shape, jnp.bfloat16)
    later = pl.pallas_call(
        functools.partial(late_kernel, layer),
        out_shape=out_shape,
        in_specs=[vmem] * 5,
        out_specs=vmem,
        compiler_params=params,
        name="late",
    )(own, lags, gain, up, down)
    return pl.pallas_call(
        functools.partial(early_kernel, layer),
        out_shape=out_shape,
        in_specs=[vmem] * 7,
        out_specs=vmem,
        scratch_shapes=[pltpu.VMEM((before + GROUP,) + own.shape[1:], jnp.bfloat16)],
        input_output_aliases={6: 0},
        compiler_params=params,
        name="early",
    )(own, halo, lags, gain, up, down, later)


def line_paths(chips):
    climb = [(2 * z, 2 * z + 2) for z in range(chips - 1)]
    sink = [(2 * z + 3, 2 * z + 1) for z in range(chips - 1)]
    forward = climb + sink + [(2 * chips - 2, 2 * chips - 1), (1, 0)]
    return forward, [(b, a) for a, b in forward]


def gather_line(state, chunks, beside=None):
    chips = lax.axis_size("zl")
    forward, backward = line_paths(chips)
    swap = lambda v: lax.ppermute(v, "co", [(0, 1), (1, 0)])
    mate = swap(state)
    ahead, behind = list(chunks), list(chunks)
    moved, joined, last = [], [], []
    for step in range(1, chips):
        for t in range(len(chunks)):
            ahead[t] = lax.ppermute(ahead[t], LINE, forward)
            behind[t] = lax.ppermute(behind[t], LINE, backward)
        moved += ahead + behind
        if step < chips - 1:
            both = join(ahead, behind, step, chips)
            if beside is not None:
                both, beside = tie(both, beside), None
            joined.append(swap(both))
        else:
            last = [swap(join(ahead, behind, step, chips))]
    return [mate, *chunks, *moved, *joined, *last]


def on_device(
    features,
    tile_cols,
    tile_weights,
    graph_gain,
    graph_up,
    graph_down,
    lag_mix,
    time_gain,
    time_up,
    time_down,
):
    snaps, vert_dev, width = features.shape
    owners = lax.axis_size(OWNERS)
    part = vert_dev // owners
    g_gain = graph_gain[:, None, :]
    t_gain = time_gain[:, None, :]
    row_tiles, k_count = tile_cols.shape[1:]
    weights = (
        tile_weights.astype(jnp.bfloat16)
        .transpose(0, 1, 3, 2, 4)
        .reshape(snaps, row_tiles, width, k_count * width)
    )
    state = features.reshape(snaps, owners, part, width)
    chunks = [state[t] for t in range(snaps)]
    for layer in range(graph_up.shape[0]):
        pieces = gather_line(state, chunks, weights if layer == 0 else None)
        graph_out = graph_stage(
            layer, tile_cols, lax.axis_size("zl"), pieces, weights, g_gain, graph_up, graph_down
        )
        owned = lax.all_to_all(graph_out, OWNERS, 0, 0, tiled=True)
        owned = owned.reshape(owners * snaps, part, width)
        finished = time_stage(layer, owned, lag_mix, t_gain, time_up, time_down)
        state = lax.all_to_all(
            finished.reshape(owners, snaps, part, width), OWNERS, 0, 0, tiled=True
        )
        chunks = [state[:, t] for t in range(snaps)]
    return state.transpose(1, 0, 2, 3).reshape(snaps, vert_dev, width)


def solution(mesh):
    fine = Mesh(mesh.devices.reshape(2, 4, 4, 4, 2), AXES)
    snap, vert = ("zh", "x", "y"), LINE
    return jax.shard_map(
        on_device,
        mesh=fine,
        in_specs=(
            P(snap, vert, None),
            P(snap, vert, None),
            P(snap, vert, None, None, None),
        )
        + (P(),) * 7,
        out_specs=P(snap, vert, None),
        check_vma=False,
    )
```

```python
import functools

import jax
import jax.numpy as jnp
from jax import lax
from jax.experimental import pallas as pl
from jax.experimental.pallas import tpu as pltpu
from jax.sharding import Mesh, PartitionSpec as P

EPS = 1e-06
AXES = ("zh", "x", "y", "zl", "co")
OWNERS = ("x", "y")
LINE = ("zl", "co")


def rms(x, gain):
    scale = lax.rsqrt(jnp.mean(x * x, axis=-1, keepdims=True) + EPS)
    return (x * scale * gain).astype(jnp.bfloat16)


def mlp(residual, rows, gain, up, down):
    x = jnp.dot(rms(rows, gain), up, preferred_element_type=jnp.float32)
    inner = x * (0.7978845608028654 + 0.035677408136300125 * (x * x))
    doubled = (x + x * jnp.tanh(inner)).astype(jnp.bfloat16)
    branch = jnp.dot(doubled, down, preferred_element_type=jnp.float32)
    return (residual.astype(jnp.float32) + 0.5 * branch).astype(jnp.bfloat16)


def graph_kernel(layer, chips, blocked, *refs):
    cols, mate = refs[:2]
    snaps, row_tiles, k_count = cols.shape
    owns = refs[2 : 2 + snaps]
    moved = refs[2 + snaps : 2 + snaps + 2 * snaps * (chips - 1)]
    rest = refs[2 + snaps + 2 * snaps * (chips - 1) :]
    joined = rest[: chips - 1]
    weights, gain, up, down, out, state, summed = rest[chips - 1 :]
    z, c = lax.axis_index("zl"), lax.axis_index("co")
    span, _, part, tile = out.shape
    per_tile = tile // part

    def place(t, slot, value):
        state[t, pl.ds(slot * span, span)] = value

    for t in range(snaps):
        place(t, 2 * z + c, owns[t][...])
        place(t, 2 * z + 1 - c, mate[:, t] if blocked else mate[t])
    for step in range(1, chips):
        ahead = moved[2 * snaps * (step - 1) : 2 * snaps * (step - 1) + snaps]
        behind = moved[2 * snaps * (step - 1) + snaps : 2 * snaps * step]
        shift = step * (1 - 2 * c)

        @pl.when(jnp.logical_and(z - shift >= 0, z - shift < chips))
        def _():
            for t in range(snaps):
                other = joined[step - 1][t if 2 * step >= chips else snaps + t]
                place(t, 2 * (z - shift) + c, ahead[t][...])
                place(t, 2 * (z - shift) + 1 - c, other)

        @pl.when(jnp.logical_and(z + shift >= 0, z + shift < chips))
        def _():
            for t in range(snaps):
                other = joined[step - 1][t]
                place(t, 2 * (z + shift) + c, behind[t][...])
                place(t, 2 * (z + shift) + 1 - c, other)

    chunk = 512
    blocks = chunk // part

    @pl.loop(0, snaps)
    def _(t):
        for r in range(row_tiles):
            picked = jnp.concatenate(
                [
                    state[t, pl.ds(per_tile * cols[t, r, k], per_tile)].reshape(tile, tile)
                    for k in range(k_count)
                ],
                axis=0,
            )
            summed[pl.ds(r * tile, tile)] = jnp.dot(
                weights[t, r], picked, preferred_element_type=jnp.float32
            )
        for q in range(row_tiles * tile // chunk):
            residual = state[t, pl.ds((2 * z + c) * span + q * blocks, blocks)]
            done = mlp(
                residual.reshape(chunk, tile),
                summed[pl.ds(q * chunk, chunk)],
                gain[layer],
                up[layer],
                down[layer],
            )
            out[pl.ds(q * blocks, blocks), t] = done.reshape(blocks, part, tile)


def graph_stage(layer, cols, chips, pieces, weights, gain, up, down):
    snaps, row_tiles, _ = cols.shape
    span, part, width = pieces[1].shape
    smem = pl.BlockSpec(memory_space=pltpu.SMEM)
    vmem = pl.BlockSpec(memory_space=pltpu.VMEM)
    return pl.pallas_call(
        functools.partial(graph_kernel, layer, chips, layer > 0),
        out_shape=jax.ShapeDtypeStruct((span, snaps, part, width), jnp.bfloat16),
        in_specs=[smem] + [vmem] * (len(pieces) + 4),
        out_specs=vmem,
        scratch_shapes=[
            pltpu.VMEM((snaps, 2 * chips * span, part, width), jnp.bfloat16),
            pltpu.VMEM((row_tiles * width, width), jnp.float32),
        ],
        compiler_params=pltpu.CompilerParams(vmem_limit_bytes=12 << 20),
        name="graph",
    )(cols, *pieces, weights, gain, up, down)


def join(ahead, behind, step, chips, after):
    snaps = len(ahead)
    one_way = 2 * step >= chips

    def kernel(*refs):
        out = refs[-1]

        def put(first, values):
            for index, value in enumerate(values):
                out[first + index] = value[...]

        if one_way:
            source = lax.axis_index("zl") - step * (1 - 2 * lax.axis_index("co"))
            from_ahead = jnp.logical_and(source >= 0, source < chips)
            pl.when(from_ahead)(lambda: put(0, refs[:snaps]))
            pl.when(jnp.logical_not(from_ahead))(lambda: put(0, refs[snaps : 2 * snaps]))
        else:
            put(0, refs[: 2 * snaps])

    count = snaps if one_way else 2 * snaps
    vmem = pl.BlockSpec(memory_space=pltpu.VMEM)
    return pl.pallas_call(
        kernel,
        out_shape=jax.ShapeDtypeStruct((count,) + ahead[0].shape, ahead[0].dtype),
        in_specs=[vmem] * (2 * snaps) + [pl.BlockSpec(memory_space=pl.ANY)],
        out_specs=vmem,
        compiler_params=pltpu.CompilerParams(vmem_limit_bytes=1 << 20),
        name="join",
    )(*ahead, *behind, after)


def tie(value, other):
    any_spec = pl.BlockSpec(memory_space=pl.ANY)
    return pl.pallas_call(
        lambda *refs: None,
        out_shape=jax.ShapeDtypeStruct(value.shape, value.dtype),
        in_specs=[any_spec] * 2,
        out_specs=any_spec,
        input_output_aliases={0: 0},
        compiler_params=pltpu.CompilerParams(vmem_limit_bytes=1 << 18),
        name="tie",
    )(value, other)


GROUP = 8


def late_kernel(layer, own, lags, gain, up, down, out):
    before = lags.shape[1] - 1
    rows, width = own.shape[1:]
    @pl.loop(1, own.shape[0] // GROUP)
    def _(q):
        mixed = jnp.zeros((GROUP, rows, width), jnp.float32)
        for m in range(before + 1):
            part = own[pl.ds(q * GROUP - m, GROUP)].astype(jnp.float32)
            mixed = mixed + lags[layer, m].reshape(1, 1, width) * part
        done = mlp(
            own[pl.ds(q * GROUP, GROUP)].reshape(GROUP * rows, width),
            mixed.reshape(GROUP * rows, width),
            gain[layer],
            up[layer],
            down[layer],
        )
        out[pl.ds(q * GROUP, GROUP)] = done.reshape(GROUP, rows, width)


def early_kernel(layer, own, halo, lags, gain, up, down, later, out, ext):
    before = halo.shape[0]
    rows, width = own.shape[1:]
    ext[pl.ds(0, before)] = jnp.where(lax.axis_index("zh") > 0, halo[...], jnp.zeros_like(halo))
    ext[pl.ds(before, GROUP)] = own[pl.ds(0, GROUP)]
    mixed = jnp.zeros((GROUP, rows, width), jnp.float32)
    for m in range(before + 1):
        part = ext[pl.ds(before - m, GROUP)].astype(jnp.float32)
        mixed = mixed + lags[layer, m].reshape(1, 1, width) * part
    done = mlp(
        own[pl.ds(0, GROUP)].reshape(GROUP * rows, width),
        mixed.reshape(GROUP * rows, width),
        gain[layer],
        up[layer],
        down[layer],
    )
    out[pl.ds(0, GROUP)] = done.reshape(GROUP, rows, width)


def time_stage(layer, own, lags, gain, up, down):
    before = lags.shape[1] - 1
    halo = lax.ppermute(own[-before:], "zh", [(0, 1), (1, 0)])
    vmem = pl.BlockSpec(memory_space=pltpu.VMEM)
    params = pltpu.CompilerParams(vmem_limit_bytes=4 << 20)
    out_shape = jax.ShapeDtypeStruct(own.shape, jnp.bfloat16)
    later = pl.pallas_call(
        functools.partial(late_kernel, layer),
        out_shape=out_shape,
        in_specs=[vmem] * 5,
        out_specs=vmem,
        compiler_params=params,
        name="late",
    )(own, lags, gain, up, down)
    return pl.pallas_call(
        functools.partial(early_kernel, layer),
        out_shape=out_shape,
        in_specs=[vmem] * 7,
        out_specs=vmem,
        scratch_shapes=[pltpu.VMEM((before + GROUP,) + own.shape[1:], jnp.bfloat16)],
        input_output_aliases={6: 0},
        compiler_params=params,
        name="early",
    )(own, halo, lags, gain, up, down, later)


def line_paths(chips):
    climb = [(2 * z, 2 * z + 2) for z in range(chips - 1)]
    sink = [(2 * z + 3, 2 * z + 1) for z in range(chips - 1)]
    forward = climb + sink + [(2 * chips - 2, 2 * chips - 1), (1, 0)]
    return forward, [(b, a) for a, b in forward]


def gather_line(state, chunks, beside=None):
    chips = lax.axis_size("zl")
    forward, backward = line_paths(chips)
    swap = lambda v: lax.ppermute(v, "co", [(0, 1), (1, 0)])
    mate = swap(state)
    ahead, behind = list(chunks), list(chunks)
    moved, joined, last = [], [], []
    for step in range(1, chips):
        for t in range(len(chunks)):
            ahead[t] = lax.ppermute(ahead[t], LINE, forward)
            behind[t] = lax.ppermute(behind[t], LINE, backward)
        moved += ahead + behind
        if step < chips - 1:
            both = join(ahead, behind, step, chips, mate)
            if beside is not None:
                both, beside = tie(both, beside), None
            joined.append(swap(both))
        else:
            last = [swap(join(ahead, behind, step, chips, mate))]
    return [mate, *chunks, *moved, *joined, *last]


def on_device(
    features,
    tile_cols,
    tile_weights,
    graph_gain,
    graph_up,
    graph_down,
    lag_mix,
    time_gain,
    time_up,
    time_down,
):
    snaps, vert_dev, width = features.shape
    owners = lax.axis_size(OWNERS)
    part = vert_dev // owners
    g_gain = graph_gain[:, None, :]
    t_gain = time_gain[:, None, :]
    row_tiles, k_count = tile_cols.shape[1:]
    weights = (
        tile_weights.astype(jnp.bfloat16)
        .transpose(0, 1, 3, 2, 4)
        .reshape(snaps, row_tiles, width, k_count * width)
    )
    state = features.reshape(snaps, owners, part, width)
    chunks = [state[t] for t in range(snaps)]
    for layer in range(graph_up.shape[0]):
        pieces = gather_line(state, chunks, weights if layer == 0 else None)
        graph_out = graph_stage(
            layer, tile_cols, lax.axis_size("zl"), pieces, weights, g_gain, graph_up, graph_down
        )
        owned = lax.all_to_all(graph_out, OWNERS, 0, 0, tiled=True)
        owned = owned.reshape(owners * snaps, part, width)
        finished = time_stage(layer, owned, lag_mix, t_gain, time_up, time_down)
        state = lax.all_to_all(
            finished.reshape(owners, snaps, part, width), OWNERS, 0, 0, tiled=True
        )
        chunks = [state[:, t] for t in range(snaps)]
    return state.transpose(1, 0, 2, 3).reshape(snaps, vert_dev, width)


def solution(mesh):
    fine = Mesh(mesh.devices.reshape(2, 4, 4, 4, 2), AXES)
    snap, vert = ("zh", "x", "y"), LINE
    return jax.shard_map(
        on_device,
        mesh=fine,
        in_specs=(
            P(snap, vert, None),
            P(snap, vert, None),
            P(snap, vert, None, None, None),
        )
        + (P(),) * 7,
        out_specs=P(snap, vert, None),
        check_vma=False,
    )
```
